256 devices in a mesh: ctx: 16 (over z, core), head: 16 (over y, x).
Axes of the slice: x: 4, y: 4, z: 8, core: 2. Of those that a mesh axis runs over, the one named last changes fastest.
Arguments:
- queries: bfloat16 [6144, 32, 128], P(('ctx', 'head')), may hold values from -52 to 52
- key_vectors: bfloat16 [6144, 32, 128], P(('ctx', 'head')), may hold values from -4 to 4
- values: bfloat16 [6144, 32, 128], P(('ctx', 'head')), may hold values from -6 to 6
- directions: bfloat16 [6144, 32, 128], P(('ctx', 'head')), may hold values from -6 to 6
- beta_logit: bfloat16 [6144, 32], P(('ctx', 'head')), may hold values from -4.5 to 9
Outputs:
- attended: bfloat16 [6144, 32, 128], P(('ctx', 'head'))
The draws below stay inside these ranges and needn't reach their ends.
All inputs are finite; a program needn't handle non-finite values.
Results may differ from the reference program's by a relative error of at most 0.0052.
Values may be sent and summed in bfloat16 or wider, within the bound.
No kernel may reach another device: no remote copies, remote signals or barrier semaphores. Data moves between devices by JAX's collectives and lax.ppermute only.
A program may use at most 64 MiB of HBM per device.

```python
import jax
import jax.numpy as jnp
from jax import lax

HEADS = 32
HEAD_DIM = 128
SUB = 64
TOK_BLK = 384
TOKEN_TOTAL = 6144


def queries_and_keys(key):
    shape = (TOKEN_TOTAL, HEADS, HEAD_DIM)
    base_keys = jax.random.fold_in(key, 11)
    base_queries = jax.random.fold_in(key, 12)
    key_rows = jnp.clip(jax.random.normal(base_keys, shape, jnp.float32), -4.0, 4.0)
    query_rows = jnp.clip(jax.random.normal(base_queries, shape, jnp.float32), -4.0, 4.0)
    return (query_rows, key_rows)


def draw_queries(key, part):
    return queries_and_keys(key)[0].astype(jnp.bfloat16)


def draw_key_vectors(key, part):
    return queries_and_keys(key)[1].astype(jnp.bfloat16)


def draw_beta_logit(key, part):
    shape = (TOKEN_TOTAL, HEADS)
    reach = jnp.log(jnp.maximum(2.0 * TOKEN_TOTAL / HEAD_DIM, 2.0))
    slow_heads = jax.random.randint(jax.random.fold_in(key, 21), (HEADS,), 0, 2) == 1
    steady = reach + 0.5 + 2.0 * jax.random.uniform(jax.random.fold_in(key, 22), shape, jnp.float32)
    quick = jnp.clip(1.5 * jax.random.normal(jax.random.fold_in(key, 23), shape, jnp.float32), -4.5, 4.5)
    score_logits = jnp.where(slow_heads[None, :], steady, quick)
    sequence_spans = jax.random.randint(jax.random.fold_in(key, 24), (TOKEN_TOTAL, 1), 0, 512) == 0
    score_logits = jnp.where(sequence_spans, 0.0, score_logits)
    return score_logits.astype(jnp.bfloat16)


def level_of(stream_key, shape, cuts, least, top_value):
    def one(axis_at, parts):
        draws = jax.random.uniform(jax.random.fold_in(jax.random.fold_in(stream_key, 6), axis_at), (parts,), jnp.float32, least / len(cuts), top_value / len(cuts))
        return jnp.repeat(jnp.exp(draws), shape[axis_at] // parts).reshape((-1,) + (1,) * (len(shape) - axis_at - 1))

    loudness = one(*cuts[0])
    for cut in cuts[1:]:
        loudness = loudness * one(*cut)
    return loudness


def gaussian(own_key, dims, scale, most, cuts=(), kind=jnp.bfloat16):
    drawn = jax.random.normal(own_key, dims, jnp.float32) * scale
    if len(cuts) > 0:
        drawn = level_of(own_key, dims, cuts, -0.22, 0.18) * drawn
    return jnp.clip(drawn, min=-most, max=most).astype(kind)


def setup_inputs(seed: int = 0) -> dict:
    splits = jax.random.split(jax.random.key(seed), 6)
    queries = draw_queries(jax.random.fold_in(splits[5], 71), 0)
    key_vectors = draw_key_vectors(jax.random.fold_in(splits[5], 71), 0)
    values = gaussian(splits[2], (TOKEN_TOTAL, HEADS, HEAD_DIM), 1.0, 6.0, ((0, 256),))
    directions = gaussian(splits[3], (TOKEN_TOTAL, HEADS, HEAD_DIM), 1.0, 6.0, ((0, 256),))
    beta_logit = draw_beta_logit(jax.random.fold_in(splits[5], 71), 0)
    return dict(queries=queries, key_vectors=key_vectors, values=values, directions=directions, beta_logit=beta_logit)


precise = lax.Precision.HIGHEST
far_below = -1e+30

def round_half(array):
    return lax.optimization_barrier(array.astype(jnp.bfloat16)).astype(jnp.float32)

def widen(array):
    return array.astype(jnp.float32)

def unit_rows(directions):
    widened = directions.astype(jnp.float32)
    return widened * lax.rsqrt(lax.optimization_barrier(jnp.sum(widened * widened, axis=-1, keepdims=True)) + 1e-06)

def sub_blocks(query_float, key_float, unit_dirs, beta_rate, sub_size):
    row_count, head_count, head_width = query_float.shape
    sub_count = row_count // sub_size
    query_sub = query_float.reshape(sub_count, sub_size, head_count, head_width)
    key_sub = key_float.reshape(sub_count, sub_size, head_count, head_width)
    dir_sub = unit_dirs.reshape(sub_count, sub_size, head_count, head_width)
    rate_sub = beta_rate.reshape(sub_count, sub_size, head_count)
    positions = lax.iota(jnp.int32, sub_size)
    strictly_lower = positions[:, None] > positions[None, :]
    lower_incl = positions[:, None] >= positions[None, :]
    identity_sub = jnp.eye(sub_size, dtype=jnp.float32)
    gram_matrix = jnp.einsum('nahe,nbhe->nhab', dir_sub, dir_sub, precision=precise)
    inv_rate = jnp.transpose(1.0 / rate_sub, (0, 2, 1))
    triangle = jnp.where(strictly_lower, gram_matrix, 0.0) + identity_sub * inv_rate[..., None]
    inverse = jax.scipy.linalg.solve_triangular(triangle, jnp.broadcast_to(identity_sub, triangle.shape), lower=True)
    query_dots = jnp.where(lower_incl, jnp.einsum('nihe,nahe->nhia', query_sub, dir_sub, precision=precise), 0.0)
    key_dots = jnp.where(strictly_lower.T, jnp.einsum('njhe,nbhe->nhjb', key_sub, dir_sub, precision=precise), 0.0)
    query_mix = jnp.einsum('nhia,nhab->nhib', query_dots, inverse, precision=precise)
    key_mix = jnp.einsum('nhjb,nhab->nhja', key_dots, inverse, precision=precise)
    inner_scores = jnp.einsum('nihe,njhe->nhij', query_sub, key_sub, precision=precise) - jnp.einsum('nhib,nhjb->nhij', query_mix, key_dots, precision=precise)
    start_query = query_sub - jnp.einsum('nhib,nbhe->nihe', query_mix, dir_sub, precision=precise)
    end_keys = key_sub - jnp.einsum('nhja,nahe->njhe', key_mix, dir_sub, precision=precise)
    transport = jnp.eye(head_width, dtype=jnp.float32) - jnp.einsum('nahe,nhab,nbhf->nhef', dir_sub, inverse, dir_sub, precision=precise)
    return (inner_scores, start_query, end_keys, transport)

def frames(inner_scores, start_query, end_keys, transport, sub_size, score_scale):
    sub_count, _, head_count, head_width = start_query.shape
    frame_count = sub_count // 2
    frame_size = 2 * sub_size
    inner_pairs = inner_scores.reshape(frame_count, 2, head_count, sub_size, sub_size)
    query_pairs = start_query.reshape(frame_count, 2, sub_size, head_count, head_width)
    key_pairs = end_keys.reshape(frame_count, 2, sub_size, head_count, head_width)
    map_pairs = transport.reshape(frame_count, 2, head_count, head_width, head_width)
    first_map = map_pairs[:, 0]
    second_map = map_pairs[:, 1]
    lifted_query = jnp.einsum('fihe,fhek->fihk', query_pairs[:, 1], first_map, precision=precise)
    pushed_keys = jnp.einsum('fjhk,fhek->fjhe', key_pairs[:, 0], second_map, precision=precise)
    framed_query_rows = jnp.concatenate([query_pairs[:, 0], lifted_query], axis=1)
    frame_keys = jnp.concatenate([pushed_keys, key_pairs[:, 1]], axis=1)
    frame_map = jnp.einsum('fhek,fhkg->fheg', second_map, first_map, precision=precise)
    cross_scores = jnp.einsum('fihe,fjhe->fhij', query_pairs[:, 1], key_pairs[:, 0], precision=precise)
    blocked = jnp.zeros_like(cross_scores)
    upper_half = jnp.concatenate([inner_pairs[:, 0], blocked], axis=-1)
    lower_half = jnp.concatenate([cross_scores, inner_pairs[:, 1]], axis=-1)
    combined_parts = jnp.concatenate([upper_half, lower_half], axis=2) * score_scale
    positions = lax.iota(jnp.int32, frame_size)
    combined_parts = jnp.where(positions[:, None] >= positions[None, :], combined_parts, far_below)
    return (combined_parts, framed_query_rows, frame_keys, frame_map)

def start_state(combined_parts, frame_values):
    frame_count, head_count, frame_size, _ = combined_parts.shape
    row_maximum = lax.optimization_barrier(jnp.max(combined_parts, axis=-1))
    weights = jnp.exp(combined_parts - row_maximum[..., None])
    row_total = lax.optimization_barrier(jnp.sum(weights, axis=-1))
    weighted = jnp.einsum('fhij,fjhe->fihe', round_half(weights), widen(frame_values), precision=precise)
    row_count = frame_count * frame_size
    row_maximum = jnp.transpose(row_maximum, (0, 2, 1)).reshape(row_count, head_count)
    row_total = jnp.transpose(row_total, (0, 2, 1)).reshape(row_count, head_count)
    weighted = weighted.reshape(row_count, head_count, weighted.shape[-1])
    return (row_maximum, row_total, weighted)

def absorb(softmax_state, scores, value_entries):
    row_maximum, row_total, weighted = softmax_state
    new_max = jnp.maximum(row_maximum, lax.optimization_barrier(jnp.max(scores, axis=-1)))
    factor = jnp.exp(row_maximum - new_max)
    weights = jnp.exp(scores - new_max[..., None])
    row_total = row_total * factor + lax.optimization_barrier(jnp.sum(weights, axis=-1))
    weighted = weighted * factor[..., None] + jnp.einsum('ihj,jhe->ihe', round_half(weights), widen(value_entries), precision=precise)
    return (new_max, row_total, weighted)

def local_block(queries, key_vectors, values, directions, beta_logit, sub_size):
    row_count, head_count, head_width = queries.shape
    score_scale = head_width ** (-0.5)
    unit_dirs = unit_rows(directions)
    beta_rate = 2.0 / (1.0 + jnp.exp(-beta_logit.astype(jnp.float32)))
    inner_scores, start_query, end_keys, transport = sub_blocks(widen(queries), widen(key_vectors), unit_dirs, beta_rate, sub_size)
    combined_parts, framed_query_rows, frame_keys, frame_map = frames(inner_scores, start_query, end_keys, transport, sub_size, score_scale)
    frame_count = combined_parts.shape[0]
    frame_size = 2 * sub_size
    frame_values = values.reshape(frame_count, frame_size, head_count, head_width)
    softmax_state = start_state(combined_parts, frame_values)
    frame_half = round_half(frame_keys)
    frame_of_row = lax.iota(jnp.int32, row_count) // frame_size
    identity_heads = jnp.broadcast_to(jnp.eye(head_width, dtype=jnp.float32), (head_count, head_width, head_width))

    def descend(running, block_index):
        current, softmax_state = running
        is_later = (frame_of_row > block_index)[:, None, None]
        scores = jnp.einsum('ihe,jhe->ihj', round_half(current), frame_half[block_index], precision=precise) * score_scale
        scores = jnp.where(is_later, scores, far_below)
        softmax_state = absorb(softmax_state, scores, frame_values[block_index])
        advanced = jnp.einsum('ihe,hek->ihk', current, frame_map[block_index], precision=precise)
        return ((jnp.where(is_later, advanced, current), softmax_state), None)
    (block_query, softmax_state), _ = lax.scan(descend, (framed_query_rows.reshape(row_count, head_count, head_width), softmax_state), jnp.arange(frame_count - 1, -1, -1, dtype=jnp.int32))

    def ascend(running, block_index):
        current, product = running
        is_earlier = (frame_of_row < block_index)[:, None, None]
        advanced = jnp.einsum('jhk,hek->jhe', current, frame_map[block_index], precision=precise)
        product = jnp.einsum('hek,hkg->heg', frame_map[block_index], product, precision=precise)
        return ((jnp.where(is_earlier, advanced, current), product), None)
    (block_keys, block_map), _ = lax.scan(ascend, (frame_keys.reshape(row_count, head_count, head_width), identity_heads), jnp.arange(frame_count, dtype=jnp.int32))
    return (softmax_state, block_query, block_keys.astype(jnp.bfloat16), block_map)

def remote_absorb(softmax_state, block_query, carried_map, key_half, value_entries, score_scale):
    moved_query = round_half(jnp.einsum('ihe,hek->ihk', block_query, carried_map, precision=precise))
    scores = jnp.einsum('ihe,jhe->ihj', moved_query, widen(key_half), precision=precise) * score_scale
    return absorb(softmax_state, scores, value_entries)

def reference(queries, key_vectors, values, directions, beta_logit):
    token_count, head_count, head_width = queries.shape
    block_count = token_count // TOK_BLK
    score_scale = head_width ** (-0.5)
    identity_one = jnp.eye(head_width, dtype=jnp.float32)[None]

    def per_head(arrays):
        head_query, head_keys, head_values, head_dirs, head_logit = arrays
        shaped = (head_query.reshape(block_count, TOK_BLK, 1, head_width), head_keys.reshape(block_count, TOK_BLK, 1, head_width), head_values.reshape(block_count, TOK_BLK, 1, head_width), head_dirs.reshape(block_count, TOK_BLK, 1, head_width), head_logit.reshape(block_count, TOK_BLK, 1))

        def one_block(pieces):
            return local_block(pieces[0], pieces[1], pieces[2], pieces[3], pieces[4], SUB)
        states, block_query, block_keys, block_map = lax.map(one_block, shaped)
        value_blocks = shaped[2]
        outputs = []
        for query_block in range(block_count):
            softmax_state = jax.tree.map(lambda leaf_array: leaf_array[query_block], states)
            if query_block > 0:
                own_query = block_query[query_block]

                def step_back(running, block_index):
                    inner_state, product = running
                    inner_state = remote_absorb(inner_state, own_query, product, block_keys[block_index], value_blocks[block_index], score_scale)
                    product = jnp.einsum('hek,hkg->heg', product, block_map[block_index], precision=precise)
                    return ((inner_state, product), None)
                (softmax_state, _), _ = lax.scan(step_back, (softmax_state, identity_one), jnp.arange(query_block - 1, -1, -1, dtype=jnp.int32))
            row_maximum, row_total, weighted = softmax_state
            outputs.append(weighted / row_total[..., None])
        return jnp.concatenate(outputs, axis=0)
    stacked = (jnp.moveaxis(queries, 1, 0)[:, :, None, :], jnp.moveaxis(key_vectors, 1, 0)[:, :, None, :], jnp.moveaxis(values, 1, 0)[:, :, None, :], jnp.moveaxis(directions, 1, 0)[:, :, None, :], jnp.moveaxis(beta_logit, 1, 0)[:, :, None])
    result = lax.map(per_head, stacked)
    return jnp.moveaxis(result[:, :, 0, :], 0, 1).astype(jnp.bfloat16)
```

```python
import functools

import jax
import jax.numpy as jnp
from jax import lax
from jax.experimental import pallas as pl
from jax.experimental.pallas import tpu as pltpu
from jax.sharding import Mesh, PartitionSpec as P

FRAME = 128
WIDTH = 128
ROWS = 768
FRAMES = ROWS // FRAME
CHUNK = 24
SOURCES = ROWS // CHUNK
SCALE = WIDTH**-0.5
HIGH = lax.Precision.HIGHEST
F32 = jnp.float32
BF16 = jnp.bfloat16


def mm(a, b):
    return lax.dot_general(a, b, (((1,), (0,)), ((), ())), precision=HIGH, preferred_element_type=F32)


def mm_t(a, b):
    return lax.dot_general(a, b, (((1,), (1,)), ((), ())), precision=HIGH, preferred_element_type=F32)


def half_t(a, b):
    return lax.dot_general(a, b, (((1,), (1,)), ((), ())), preferred_element_type=F32)


def half(a, b):
    return lax.dot_general(a, b, (((1,), (0,)), ((), ())), preferred_element_type=F32)


def frame_of(index):
    return pl.ds(index * FRAME, FRAME)


def key_kernel(first_ref, dirs_ref, mixed_ref, key_mix_ref, frame_half_ref, half_ref, maps_ref, map_ref):
    raw = first_ref[:, 0:CHUNK, :].reshape(ROWS, WIDTH).astype(F32)
    unit = raw * lax.rsqrt(jnp.sum(raw * raw, axis=1, keepdims=True) + 1e-06)
    dirs_ref[...] = unit
    keys = first_ref[:, CHUNK : 2 * CHUNK, :].reshape(ROWS, WIDTH).astype(F32)

    token = lax.broadcasted_iota(jnp.int32, (ROWS, SOURCES), 0)
    source = lax.broadcasted_iota(jnp.int32, (ROWS, SOURCES), 1)
    chosen = ((token >= source * CHUNK) & (token < (source + 1) * CHUNK)).astype(F32).astype(BF16)
    spread = half(chosen, first_ref[:, 2 * CHUNK, :])
    token = lax.broadcasted_iota(jnp.int32, (ROWS, WIDTH), 0)
    place = token - lax.shift_right_logical(token * 2731, 16) * CHUNK
    lane = lax.broadcasted_iota(jnp.int32, (ROWS, WIDTH), 1)
    logit = jnp.sum(jnp.where(place == lane, spread, 0.0), axis=1, keepdims=True)
    rate = 2.0 / (1.0 + jnp.exp(-logit))

    row = lax.broadcasted_iota(jnp.int32, (FRAME, FRAME), 0)
    col = lax.broadcasted_iota(jnp.int32, (FRAME, FRAME), 1)
    eye = (row == col).astype(F32)
    units = [unit[f * FRAME : (f + 1) * FRAME] for f in range(FRAMES)]
    gram = [jnp.where(row > col, mm_t(u, u), 0.0) for u in units]
    inverse = []
    for f in range(FRAMES):
        rate_col = rate[f * FRAME : (f + 1) * FRAME]
        rate_row = jnp.sum(eye * rate_col, axis=0, keepdims=True)
        pair = (lax.shift_right_logical(row, 1) == lax.shift_right_logical(col, 1)).astype(F32)
        inverse.append(eye * rate_col - pair * gram[f] * rate_col * rate_row)
    level = 1
    while (2 << level) <= FRAME:
        joined = (
            lax.shift_right_logical(row, level + 1) == lax.shift_right_logical(col, level + 1)
        ) & (lax.shift_right_logical(row, level) != lax.shift_right_logical(col, level))
        left = [mm(inverse[f], jnp.where(joined, gram[f], 0.0)) for f in range(FRAMES)]
        inverse = [inverse[f] - mm(left[f], inverse[f]) for f in range(FRAMES)]
        level += 1
    frame_maps = []
    frame_keys = []
    for f in range(FRAMES):
        own = keys[f * FRAME : (f + 1) * FRAME]
        mixed = mm(inverse[f], units[f])
        mixed_ref[frame_of(f), :] = mixed
        frame_map = eye - mm(units[f].T, mixed)
        maps_ref[frame_of(f), :] = frame_map
        frame_maps.append(frame_map)
        key_dots = jnp.where(col > row, mm_t(own, units[f]), 0.0)
        key_mix = mm_t(key_dots, inverse[f])
        key_mix_ref[frame_of(f), :] = key_mix
        end_keys = own - mm(key_mix, units[f])
        frame_half_ref[frame_of(f), :] = end_keys.astype(BF16)
        frame_keys.append(end_keys)
    after = [None] * FRAMES
    after[4] = frame_maps[5]
    after[3] = mm(frame_maps[5], frame_maps[4])
    middle = mm(frame_maps[3], frame_maps[2])
    first = mm(frame_maps[1], frame_maps[0])
    after[2] = mm(after[3], frame_maps[3])
    after[1] = mm(after[3], middle)
    after[0] = mm(after[1], frame_maps[1])
    map_ref[...] = mm(after[1], first)
    for f in range(FRAMES):
        moved = frame_keys[f] if after[f] is None else mm_t(frame_keys[f], after[f])
        half_ref[frame_of(f), :] = moved.astype(BF16)


def query_kernel(
    first_ref, second_ref, dirs_ref, mixed_ref, key_mix_ref, frame_half_ref, maps_ref,
    query_ref, top_ref, total_ref, sum_ref, score_ref, value_ref,
):
    row = lax.broadcasted_iota(jnp.int32, (FRAME, FRAME), 0)
    col = lax.broadcasted_iota(jnp.int32, (FRAME, FRAME), 1)
    queries = second_ref[:, 0:CHUNK, :].reshape(ROWS, WIDTH)
    keys = first_ref[:, CHUNK : 2 * CHUNK, :].reshape(ROWS, WIDTH)
    value_ref[...] = second_ref[:, CHUNK : 2 * CHUNK, :].reshape(ROWS, WIDTH)
    for f in range(FRAMES):
        own = queries[f * FRAME : (f + 1) * FRAME]
        own_float = own.astype(F32)
        dots = jnp.where(row >= col, mm_t(own_float, dirs_ref[frame_of(f), :]), 0.0)
        query_ref[frame_of(f), :] = own_float - mm(dots, mixed_ref[frame_of(f), :])
        inner = half_t(own, keys[f * FRAME : (f + 1) * FRAME]) - mm_t(dots, key_mix_ref[frame_of(f), :])
        score_ref[frame_of(f), frame_of(f)] = jnp.where(row >= col, inner * SCALE, -1e30)
    for g in range(FRAMES - 2, -1, -1):
        later = pl.ds((g + 1) * FRAME, (FRAMES - 1 - g) * FRAME)
        current = query_ref[later, :]
        score_ref[later, frame_of(g)] = half_t(current.astype(BF16), frame_half_ref[frame_of(g), :]) * SCALE
        query_ref[later, :] = mm(current, maps_ref[frame_of(g), :])
    for f in range(FRAMES):
        seen = (f + 1) * FRAME
        scores = score_ref[frame_of(f), 0:seen]
        top = jnp.max(scores, axis=1, keepdims=True)
        weights = jnp.exp(scores - top)
        top_ref[frame_of(f), :] = jnp.broadcast_to(top, (FRAME, WIDTH))
        total_ref[frame_of(f), :] = jnp.broadcast_to(jnp.sum(weights, axis=1, keepdims=True), (FRAME, WIDTH))
        sum_ref[frame_of(f), :] = half(weights.astype(BF16), value_ref[0:seen, :])


def attend_kernel(plan, tile, last, *refs):
    map_count = 1 + max([m for m, _ in plan if m is not None], default=-1)
    block_count = 1 + max([b for _, b in plan if b is not None], default=-1)
    refs = list(refs)
    valid_ref = refs.pop(0)
    query_ref, top_in, total_in, sum_in = refs[:4]
    maps = refs[4 : 4 + map_count]
    keys = refs[4 + map_count : 4 + map_count + block_count]
    values = refs[4 + map_count + block_count : 4 + map_count + 2 * block_count]
    outs = refs[4 + map_count + 2 * block_count :]
    if last:
        out_ref, top_ref, total_ref, sum_ref, moved_ref = outs
    else:
        moved_ref, top_ref, total_ref, sum_ref = outs
    for t in range(ROWS // tile):
        rows = pl.ds(t * tile, tile)
        top_ref[rows, :] = top_in[rows, :]
        total_ref[rows, :] = total_in[rows, :]
        sum_ref[rows, :] = sum_in[rows, :]
        moved_ref[rows, :] = query_ref[rows, :]
    for map_index, block in plan:
        flag = valid_ref[0 if block is None else block]

        def step(map_index=map_index, block=block):
            for t in range(ROWS // tile):
                rows = pl.ds(t * tile, tile)
                current = moved_ref[rows, :]
                if map_index is not None:
                    current = mm(current, maps[map_index][...])
                    moved_ref[rows, :] = current
                if block is None:
                    continue
                scores = half_t(current.astype(BF16), keys[block][...]) * SCALE
                top = top_ref[rows, 0:1]
                new_top = jnp.maximum(top, jnp.max(scores, axis=1, keepdims=True))
                factor = jnp.exp(top - new_top)
                weights = jnp.exp(scores - new_top)
                top_ref[rows, :] = jnp.broadcast_to(new_top, (tile, WIDTH))
                total_ref[rows, :] = total_ref[rows, :] * factor + jnp.sum(weights, axis=1, keepdims=True)
                sum_ref[rows, :] = sum_ref[rows, :] * factor + half(weights.astype(BF16), values[block][...])

        pl.when(flag > 0)(step)
    if last:
        out_ref[...] = (sum_ref[...] / total_ref[...]).astype(BF16).reshape(SOURCES, CHUNK, WIDTH)


def sds(shape, dtype):
    return jax.ShapeDtypeStruct(shape, dtype)


VM = pl.BlockSpec(memory_space=pltpu.VMEM)
SM = pl.BlockSpec(memory_space=pltpu.SMEM)
STATE = (ROWS, WIDTH)


def cost(flops, nbytes):
    return pl.CostEstimate(flops=flops, bytes_accessed=nbytes, transcendentals=0)


def run_keys(first):
    return pl.pallas_call(
        key_kernel,
        out_shape=(
            sds(STATE, F32), sds(STATE, F32), sds(STATE, F32), sds(STATE, BF16), sds(STATE, BF16),
            sds(STATE, F32), sds((WIDTH, WIDTH), F32),
        ),
        in_specs=[VM],
        out_specs=(VM,) * 7,
        name="key_side",
        cost_estimate=cost(6 * 20 * 6 * 2 * 128**3, 4_000_000),
    )(first)


def run_queries(first, second, *parts):
    return pl.pallas_call(
        query_kernel,
        out_shape=(sds(STATE, F32),) * 4,
        in_specs=[VM] * 7,
        out_specs=(VM,) * 4,
        scratch_shapes=[pltpu.VMEM((ROWS, ROWS), F32), pltpu.VMEM(STATE, BF16)],
        name="query_side",
        cost_estimate=cost(6 * 20 * 6 * 2 * 128**3, 4_000_000),
    )(first, second, *parts)


def run_attend(plan, valid, state, maps, keys, values, last=False):
    state_out = (sds(STATE, F32),) * 4
    operands = (valid, *state, *maps, *keys, *values)
    if last:
        out_shape, out_specs = sds((SOURCES, CHUNK, WIDTH), BF16), VM
        scratch = [pltpu.VMEM(STATE, F32)] * 4
    else:
        out_shape, out_specs, scratch = state_out, (VM,) * 4, []
    return pl.pallas_call(
        functools.partial(attend_kernel, plan, 256, last),
        out_shape=out_shape,
        in_specs=[SM] + [VM] * (len(operands) - 1),
        out_specs=out_specs,
        scratch_shapes=scratch,
        name="attend_" + str(len(keys)) + ("_last" if last else ""),
        cost_estimate=cost(len(keys) * 4_000_000_000, 4_000_000),
    )(*operands)


def shards(queries, key_vectors, values, directions, beta_logit):
    ring = lax.axis_size("z")
    own = lax.axis_index("z")

    def hop(value, by):
        return lax.ppermute(value, "z", [(i, (i + by) % ring) for i in range(ring)])

    def by_head(array):
        return jnp.swapaxes(array, 0, 1)

    logits = jnp.pad(by_head(beta_logit)[:, None, :], ((0, 0), (0, 7), (0, WIDTH - CHUNK)))
    first = jnp.concatenate([by_head(directions), by_head(key_vectors), logits], axis=1)
    second = jnp.concatenate([by_head(queries), by_head(values)], axis=1)
    first = lax.all_to_all(first, ("core", "head"), 0, 0, tiled=True)
    second = lax.all_to_all(second, ("core", "head"), 0, 0, tiled=True)

    value0 = second[:, CHUNK:, :].reshape(STATE)
    dirs, mixed, key_mix, frame_half, key0, maps, map0 = run_keys(first)
    query, top, total, acc = run_queries(first, second, dirs, mixed, key_mix, frame_half, maps)

    ahead = {"k": [key0], "v": [value0], "m": [map0]}
    back = {"k": [key0], "v": [value0], "m": [map0]}
    for _ in range(4):
        for name in ("m", "k", "v"):
            ahead[name].append(hop(ahead[name][-1], 1))
    for index in range(3):
        for name in ("m", "k", "v"):
            if name == "m" and index == 0:
                back["m"].append(hop(map0, -1))
            else:
                back[name].append(hop(back[name][-1], -1))

    def valid(*steps):
        return jnp.stack([(own >= d).astype(jnp.int32) for d in steps])

    state = (query, top, total, acc)
    state = run_attend(((None, 0),), valid(1), state, [], [ahead["k"][1]], [ahead["v"][1]])
    state = run_attend(
        ((0, 0), (1, 1)), valid(2, 3), state, ahead["m"][1:3], ahead["k"][2:4], ahead["v"][2:4]
    )
    fourth = run_map(state[0], ahead["m"][3])
    later = run_attend(
        ((0, None), (1, 0), (2, 1)) if False else ((0, 0), (1, 1), (2, 2)),
        valid(5, 6, 7),
        (fourth, *state[1:]),
        [ahead["m"][4], back["m"][3], back["m"][2]],
        [back["k"][3], back["k"][2], back["k"][1]],
        [back["v"][3], back["v"][2], back["v"][1]],
    )
    out = run_attend(
        ((None, 0),), valid(4), (fourth, *later[1:]), [], [ahead["k"][4]], [ahead["v"][4]], last=True
    )
    returned = lax.all_to_all(out, ("core", "head"), 0, 0, tiled=True)
    return jnp.swapaxes(returned, 0, 1)


def map_kernel(query_ref, map_ref, out_ref):
    out_ref[...] = mm(query_ref[...], map_ref[...])


def run_map(query, chain_map):
    return pl.pallas_call(
        map_kernel, out_shape=sds(STATE, F32), in_specs=[VM] * 2, out_specs=VM, name="move",
        cost_estimate=cost(6 * 12 * 2 * 128**3, 1_000_000),
    )(query, chain_map)


def solution(mesh):
    devices = mesh.devices.reshape(mesh.devices.shape[0] // 2, 2, mesh.devices.shape[1])
    view = Mesh(devices, ("z", "core", "head"))
    spread = ("z", "core", "head")
    in_specs = (P(spread, None, None),) * 4 + (P(spread, None),)
    return jax.shard_map(
        shards, mesh=view, in_specs=in_specs, out_specs=P(spread, None, None), check_vma=False
    )
```
